512 devices in a mesh: dp: 4 (over x), ep: 128 (over z, y, core).
Axes of the slice: x: 4, y: 8, z: 8, core: 2. Of those that a mesh axis runs over, the one named last changes fastest.
Arguments:
- tokens: bfloat16 [128, 16, 2048], P('ep', 'dp'), may hold values from -6 to 6
- dest_ids: int32 [128, 16, 8], P('ep', 'dp'), may hold values from 0 to 127, all different within a row; in each aligned block of 16 rows (0 to 15, 16 to 31, ..., all dimensions but the last counted through in order) at most 2 rows name the same one
- gate_fixed: int32 [128, 16, 8], P('ep', 'dp'), may hold values from 1 to 65535
- gate_up: bfloat16 [128, 2, 768, 2048], P('ep', None, 'dp'), may hold values from -0.125 to 0.125
- down: bfloat16 [128, 768, 2048], P('ep', 'dp'), may hold values from -0.21875 to 0.21875
Outputs:
- mixed: bfloat16 [128, 16, 2048], P('ep', 'dp')
The draws below stay inside these ranges and needn't reach their ends.
Inputs may be any that keep to these rules, and one draw needn't show every extreme that they name: `dest_ids`: each row names 8 different experts; within one column's 16 rows no expert is named by more than 2 routes.
All inputs are finite; a program needn't handle non-finite values.
Results may differ from the reference program's by a relative error of at most 0.012.
Values may be sent and summed in bfloat16 or wider, within the bound.
A program may use at most 192 MiB of HBM per device.

```python
import math
import jax
import jax.numpy as jnp
import numpy as np
from jax import lax

D = 2048
FF = 768
TOP = 8
COLUMNS = 128
EXPERTS = 128
COL_ROWS = 16
CAP = 2
N_DP = 4
N_EP = 128


def with_ends(values, key, least, high):
    shape = values.shape
    place = [jax.random.randint(jax.random.fold_in(key, axis), (), 0, shape[axis]) for axis in range(len(shape))]
    values = values.at[tuple(place)].set(least)
    longest = shape.index(max(shape))
    place[longest] = (place[longest] + 1) % shape[longest]
    return values.at[tuple(place)].set(high)


def shard_levels(key, dims, cuts, low, high):
    def one(dim, blocks):
        heights = jax.random.uniform(jax.random.fold_in(jax.random.fold_in(key, 6), dim), (blocks,), jnp.float32, low / len(cuts), high / len(cuts))
        return jnp.repeat(jnp.exp(heights), dims[dim] // blocks).reshape((-1,) + (1,) * (len(dims) - dim - 1))

    level = one(*cuts[0])
    for cut in cuts[1:]:
        level = level * one(*cut)
    return level


def assign_block(own_key, own, number, rows, amount, top, reach, slope):
    order = jax.random.permutation(own_key, amount)
    crowded, common = load_shares(amount, rows * top, reach, slope, True), load_shares(amount, rows * top, reach, slope, False)
    places = jnp.arange(amount)

    def named(lengths, offset_by):
        used = int((lengths > 0).sum())
        fixed = max(1, used // 4)
        shifted = fixed + (places - fixed + offset_by * (used - fixed)) % max(1, amount - fixed)
        return jnp.zeros((amount,), jnp.int32).at[order[jnp.where(places < fixed, places, shifted)]].set(jnp.asarray(lengths, jnp.int32))

    lengths = jnp.where(number % 4 == 0, named(crowded, number // 4), named(common, number - number // 4 - 1))
    mixed = jax.random.permutation(jax.random.fold_in(own, 3), amount)
    giver, sink = mixed[0:amount // 2 * 2:2], mixed[1:amount // 2 * 2:2]
    margin = jnp.minimum(lengths[giver] - 1, reach - lengths[sink]) // 2
    margin = jnp.where((giver == order[0]) | (sink == order[0]) | (lengths[sink] == 0), 0, jnp.maximum(margin, 0))
    shifted = jax.random.randint(jax.random.fold_in(own, 4), (amount // 2,), 0, 1 << 20) % (margin + 1)
    lengths = lengths.at[giver].add(-shifted).at[sink].add(shifted)
    items = jnp.searchsorted(jnp.cumsum(lengths), jnp.arange(rows * top), side="right").astype(jnp.int32)
    table = items.reshape(top, rows).T
    table = table[jax.random.permutation(jax.random.fold_in(own, 1), rows)]
    offset_by = jax.random.randint(jax.random.fold_in(own, 2), (rows, 1), 0, top)
    return jnp.take_along_axis(table, (jnp.arange(top)[None, :] + offset_by) % top, axis=1)


def load_shares(count, total, limit, slope, full):
    weights = [(1 << 20) // math.isqrt(standing ** slope) + 1 for standing in range(1, count + 1)]
    largest = limit if full else min(limit, max(-(-total // count), total * weights[0] // sum(weights)))
    least = 1 if total - largest >= count - 1 else 0
    given, surplus = [largest] + [least] * (count - 1), total - largest - least * (count - 1)
    while surplus > 0:
        free = [i for i in range(1, count) if given[i] < largest] or [i for i in range(1, count) if given[i] < limit]
        pool, budget = sum([weights[i] for i in free]), surplus
        for i in free:
            more = min(limit - given[i], max(1, budget * weights[i] // pool), surplus)
            given[i] = given[i] + more
            surplus = surplus - more
    return np.array(given)


def bell_draw(stream_key, dims, deviation, bound, shards=(), kind=jnp.bfloat16):
    drawn = deviation * jax.random.normal(stream_key, dims, jnp.float32)
    if shards:
        drawn = drawn * shard_levels(stream_key, dims, shards, -0.22, 0.18)
    return jnp.clip(drawn, -bound, bound).astype(kind)


def setup_inputs(seed: int = 0) -> dict:
    keys = jax.random.split(jax.random.key(seed), 6)
    tokens = bell_draw(keys[0], (COLUMNS, COL_ROWS, D), 1.0, 6.0, ((0, 128), (1, 4)))
    dest_ids_keys = jax.random.split(jax.random.fold_in(keys[1], 1), COLUMNS * COL_ROWS // COL_ROWS)
    dest_ids_turns = jax.random.permutation(jax.random.fold_in(keys[1], 3), COLUMNS * COL_ROWS // COL_ROWS)
    dest_ids = jax.vmap(lambda own, number: assign_block(jax.random.fold_in(keys[1], 2), own, number, COL_ROWS, COLUMNS, TOP, CAP, 2))(dest_ids_keys, dest_ids_turns).reshape((COLUMNS, COL_ROWS, TOP))
    gate_fixed = with_ends(jax.random.randint(keys[2], (COLUMNS, COL_ROWS, TOP), 1, 65536), jax.random.fold_in(keys[2], 1), 1, 65535).astype(jnp.int32)
    gate_up = bell_draw(keys[3], (EXPERTS, 2, FF, D), D ** -0.5, 0.125, ((0, 128), (2, 4)))
    down = bell_draw(keys[4], (EXPERTS, FF, D), FF ** -0.5, 0.21875, ((0, 128), (1, 4)))
    return dict(tokens=tokens, dest_ids=dest_ids, gate_fixed=gate_fixed, gate_up=gate_up, down=down)


def feed_forward(rows, pair, lower):
    gate = jnp.dot(rows, pair[0].T, preferred_element_type=jnp.float32)
    upper = jnp.dot(rows, pair[1].T, preferred_element_type=jnp.float32)
    hidden = (jax.nn.silu(gate) * upper).astype(jnp.bfloat16)
    quarter = hidden.shape[1] // N_DP
    pieces = jnp.einsum("nsh,shd->nsd", hidden.astype(jnp.float32).reshape(-1, N_DP, quarter),
                        lower.astype(jnp.float32).reshape(N_DP, quarter, -1),
                        precision=lax.Precision.HIGHEST)
    pieces = lax.optimization_barrier(pieces.astype(jnp.bfloat16))
    return jnp.sum(pieces.astype(jnp.float32), axis=1)


def reference(tokens, dest_ids, gate_fixed, gate_up, down):
    flat_target = dest_ids.reshape(COLUMNS, COL_ROWS * TOP)
    marks = (flat_target[:, :, None] == jnp.arange(N_EP, dtype=jnp.int32)[None, None, :]).astype(jnp.int32)
    slot_rank = jnp.sum(jnp.cumsum(marks, axis=1) * marks, axis=2) - 1
    slot_index = flat_target * CAP + slot_rank
    column_ids = jnp.broadcast_to(jnp.arange(COLUMNS, dtype=jnp.int32)[:, None], slot_index.shape)
    source_row = jnp.broadcast_to((jnp.arange(COL_ROWS * TOP, dtype=jnp.int32) // TOP)[None, :], slot_index.shape)
    row_table = jnp.zeros((COLUMNS, N_EP * CAP), jnp.int32).at[column_ids, slot_index].set(source_row)
    live_table = jnp.zeros((COLUMNS, N_EP * CAP), jnp.int32).at[column_ids, slot_index].set(1)
    column_part = column_ids[:, :CAP]

    def per_device(device):
        start = (device * CAP).astype(jnp.int32)
        rows_at = lax.dynamic_slice_in_dim(row_table, start, CAP, 1)
        live = lax.dynamic_slice_in_dim(live_table, start, CAP, 1)
        gathered = tokens[column_part, rows_at]
        gathered = jnp.where(live[:, :, None] == 1, gathered, jnp.zeros_like(gathered)).reshape(-1, D)
        own_out = feed_forward(gathered, gate_up[device], down[device])
        return own_out.reshape(COLUMNS, CAP, D)

    results = lax.map(per_device, jnp.arange(N_EP, dtype=jnp.int32))
    values = results[flat_target, column_ids, slot_rank]
    weights = gate_fixed.astype(jnp.float32)
    weights = weights / jnp.sum(weights, axis=2, keepdims=True)
    mixed = jnp.sum(values.reshape(COLUMNS, COL_ROWS, TOP, D) * weights[..., None], axis=2)
    return mixed.astype(jnp.bfloat16)
```

```python
import jax
import jax.numpy as jnp
from jax import lax
from jax.sharding import PartitionSpec as P


def feed_forward(rows, pair, lower):
    gate = jnp.einsum("nd,hd->nh", rows, pair[0], preferred_element_type=jnp.float32)
    upper = jnp.einsum("nd,hd->nh", rows, pair[1], preferred_element_type=jnp.float32)
    hidden = (jax.nn.silu(gate) * upper).astype(jnp.bfloat16)
    return jnp.dot(hidden, lower, preferred_element_type=jnp.float32).astype(jnp.bfloat16)


def per_device(tokens, dest_ids, gate_fixed, gate_up, down):
    peer_count = lax.axis_size("ep")
    own_rows = tokens[0]
    width = own_rows.shape[1]
    top_count = dest_ids.shape[2]
    gates = gate_fixed[0]
    route_table = jnp.concatenate([dest_ids[0], gates >> 8, gates & 255], axis=1)
    route_pad = jnp.pad(route_table, ((0, 0), (0, 128 - 3 * top_count))).astype(jnp.bfloat16)
    packed = lax.all_gather(jnp.concatenate([own_rows, route_pad], axis=1), "dp", axis=0, tiled=True)
    column_rows = packed[:, :width]
    table = packed[:, width : width + 3 * top_count].astype(jnp.int32)
    column_table = jnp.concatenate(
        [table[:, :top_count], table[:, top_count : 2 * top_count] * 256 + table[:, 2 * top_count :]],
        axis=1,
    )
    col_rows = column_table.shape[0]
    capacity = min(col_rows, max(2, 2 * col_rows * top_count // peer_count))
    target_dev = column_table[:, :top_count].reshape(-1)
    gate_raw = column_table[:, top_count:].astype(jnp.float32)
    gate_norm = gate_raw / jnp.sum(gate_raw, axis=1, keepdims=True)
    marks = (target_dev[:, None] == jnp.arange(peer_count, dtype=jnp.int32)[None, :]).astype(
        jnp.int32
    )
    slot_rank = jnp.sum(jnp.cumsum(marks, axis=0) * marks, axis=1) - 1
    slot_index = target_dev * capacity + slot_rank
    source_row = jnp.arange(target_dev.shape[0], dtype=jnp.int32) // top_count
    send_block = (
        jnp.zeros((peer_count * capacity, width), jnp.bfloat16)
        .at[slot_index]
        .set(column_rows[source_row])
        .reshape(peer_count, capacity, width)
    )
    rows = lax.all_to_all(send_block, "ep", split_axis=0, concat_axis=0, tiled=True)
    flat_rows = rows.reshape(-1, rows.shape[2])
    own_out = feed_forward(flat_rows, gate_up[0], down[0])
    returned = lax.all_to_all(
        own_out.reshape(rows.shape[0], rows.shape[1], -1),
        "ep",
        split_axis=0,
        concat_axis=0,
        tiled=True,
    )
    flat_back = returned.reshape(peer_count * capacity, -1)
    weighted = flat_back[slot_index].astype(jnp.float32) * gate_norm.reshape(-1)[:, None]
    summed = jnp.sum(weighted.reshape(col_rows, top_count, -1), axis=1)
    parts = lax.all_to_all(
        summed.astype(jnp.bfloat16).reshape(4, -1, width), "dp", split_axis=0, concat_axis=0, tiled=True
    )
    mine = jnp.sum(parts.astype(jnp.float32), axis=0).astype(jnp.bfloat16)
    return mine[None]


def solution(mesh):
    return jax.shard_map(
        per_device,
        mesh=mesh,
        in_specs=(
            P("ep", "dp", None),
            P("ep", "dp", None),
            P("ep", "dp", None),
            P("ep", None, "dp", None),
            P("ep", "dp", None),
        ),
        out_specs=P("ep", "dp", None),
        check_vma=False,
    )
```

```python
import jax
import jax.numpy as jnp
from jax import lax
from jax.experimental import pallas as pl
from jax.experimental.pallas import tpu as pltpu
from jax.sharding import PartitionSpec as P

BF = jnp.bfloat16
F32 = jnp.float32
MESH = pl.DeviceIdType.MESH
PEERS = 128
DP = 4
TOP = 8
LANES = 128
QUARTER = 512
BLOCKS = PEERS // 16


def iota(shape, dim):
    return lax.broadcasted_iota(jnp.int32, shape, dim)


def permutation(inverse):
    moved = iota((128, 128), 1 if inverse else 0)
    place = iota((128, 128), 0 if inverse else 1)
    home = (moved & 31) // 2 * 8 + (moved & 1) * 4 + moved // 32
    return jnp.where(home == place, 1.0, 0.0).astype(BF)


def remote(src, dst, send_sem, recv_sem, device):
    return pltpu.make_async_remote_copy(
        src_ref=src, dst_ref=dst, send_sem=send_sem, recv_sem=recv_sem,
        device_id=device, device_id_type=MESH,
    )


def kernel(
    msg_ref, pair_hbm, lower_hbm, out_ref,
    got, pair, lower, send1, recv1, rows, part, pin, send2, back, outp, fin,
    local_sem, xs, xr, a_send, a_recv, gs, gr, rs, rr, b_send, b_recv, fs, fr, own_sem,
):
    q = lax.axis_index("dp")
    me = lax.axis_index("ep")
    load_pair = pltpu.make_async_copy(pair_hbm, pair, local_sem.at[0])
    load_lower = pltpu.make_async_copy(lower_hbm, lower, local_sem.at[1])
    load_pair.start()
    load_lower.start()

    barrier = pltpu.get_barrier_semaphore()
    for d in range(1, DP):
        pl.semaphore_signal(
            barrier, inc=1, device_id={"dp": lax.rem(q + d, DP)}, device_id_type=MESH
        )

    def greet(d, carry):
        pl.semaphore_signal(
            barrier, inc=1, device_id={"ep": lax.rem(me + d, PEERS)}, device_id_type=MESH
        )
        return carry

    lax.fori_loop(1, PEERS, greet, 0)
    pl.semaphore_wait(barrier, DP - 1 + PEERS - 1)

    copies = []
    for d in range(1, DP):
        to = lax.rem(q + d, DP)
        copies.append(
            remote(msg_ref.at[to], got.at[q], xs.at[d - 1], xr.at[d - 1], {"dp": to})
        )
        copies[-1].start()
    got[q] = msg_ref[q]
    for copy in copies:
        copy.wait()

    tok = jnp.concatenate([got[i, 0:16, :] for i in range(DP)], axis=0)
    table = jnp.concatenate([got[i, 16:32, :].astype(F32) for i in range(DP)], axis=0)
    wide = (64, PEERS * 8)
    column = iota(wide, 1)
    expert = (column // 8).astype(F32)
    named = jnp.zeros(wide, F32)
    high = jnp.zeros(wide, F32)
    low = jnp.zeros(wide, F32)
    total = jnp.zeros((64, 1), F32)
    for k in range(TOP):
        same = table[:, k : k + 1] == expert
        hi, lo = table[:, TOP + k : TOP + k + 1], table[:, 2 * TOP + k : 2 * TOP + k + 1]
        total = total + (hi * 256.0 + lo)
        named = jnp.where(same, 1.0, named)
        high = jnp.where(same, hi, high)
        low = jnp.where(same, lo, low)
    earlier = jnp.where(
        (iota((64, 64), 1) // 4 < iota((64, 64), 0) // 4) & ((iota((64, 64), 1) & 3) == 0), 1.0, 0.0
    ).astype(BF)
    rank = jnp.dot(earlier, named.astype(BF), preferred_element_type=F32)
    slot = ((column // 4) & 1).astype(F32)
    live = (rank == slot) & ((iota(wide, 0) & 3) == (column & 3))
    pick = jnp.where(live, named, 0.0)
    high = jnp.where(live, high, 0.0).astype(BF)
    low = jnp.where(live, low, 0.0).astype(BF)
    packed = jnp.dot(pick.T.astype(BF), tok, preferred_element_type=F32)
    send1[...] = packed.reshape(PEERS, 8, LANES).astype(BF)

    def dispatch(d, carry):
        to = lax.rem(me + d, PEERS)
        remote(send1.at[to], recv1.at[q, me], a_send, a_recv, {"ep": to}).start()
        return carry

    lax.fori_loop(1, PEERS, dispatch, 0)
    own = pltpu.make_async_copy(send1.at[me], recv1.at[q, me], own_sem.at[0])
    own.start()
    own.wait()
    whole = pl.ds(0, PEERS - 1)
    arrived = remote(
        send1.at[whole], recv1.at[q, whole], a_send, a_recv, {"ep": lax.rem(me + 1, PEERS)}
    )
    arrived.wait()

    copies = {}
    for d in (2, 1, 3):
        to = lax.rem(q + d, DP)
        copies[d] = remote(recv1.at[q], recv1.at[q], gs.at[d - 1], gr.at[d - 1], {"dp": to})
        copies[d].start()
    load_pair.wait()
    order = permutation(False)
    gate = jnp.zeros((PEERS * 2, pair.shape[1]), F32)
    upper = jnp.zeros((PEERS * 2, pair.shape[1]), F32)
    contract = (((1,), (1,)), ((), ()))
    for d in (0, 1, 3, 2):
        if d:
            copies[d].wait()
        src = lax.rem(q + DP - d, DP)
        for b in range(BLOCKS):
            block = recv1[src, b * 16 : (b + 1) * 16].astype(F32).reshape(128, LANES).astype(BF)
            moved = jnp.dot(order, block, preferred_element_type=F32).astype(BF)
            for j in range(4):
                rows[b * 32 : (b + 1) * 32, j * LANES : (j + 1) * LANES] = moved[j * 32 : (j + 1) * 32]
        x = rows[...]
        features = pl.ds(pl.multiple_of(src * QUARTER, QUARTER), QUARTER)
        gate = gate + lax.dot_general(x, pair[0, :, features], contract, preferred_element_type=F32)
        upper = upper + lax.dot_general(x, pair[1, :, features], contract, preferred_element_type=F32)
    hidden = (gate / (1.0 + jnp.exp(-gate)) * upper).astype(BF)
    load_lower.wait()

    copies = {}
    for d in (2, 1, 3, 0):
        to = lax.rem(q + d, DP)
        features = pl.ds(pl.multiple_of(to * QUARTER, QUARTER), QUARTER)
        part[to] = jnp.dot(hidden, lower[:, features], preferred_element_type=F32).astype(BF)
        if d:
            copies[d] = remote(part.at[to], pin.at[q], rs.at[d - 1], rr.at[d - 1], {"dp": to})
            copies[d].start()
    for d in (1, 3, 2):
        copies[d].wait()
    back_order = permutation(True)
    for b in range(BLOCKS):
        lines = slice(b * 32, (b + 1) * 32)
        added = part[q, lines].astype(F32)
        for d in range(1, DP):
            added = added + pin[lax.rem(q + DP - d, DP), lines].astype(F32)
        added = added.astype(BF)
        stacked = jnp.concatenate([added[:, j * LANES : (j + 1) * LANES] for j in range(4)], axis=0)
        moved = jnp.dot(back_order, stacked, preferred_element_type=F32)
        send2[b * 16 : (b + 1) * 16] = moved.reshape(16, 8, LANES).astype(BF)

    def giveback(d, carry):
        to = lax.rem(me + d, PEERS)
        remote(send2.at[to], back.at[me], b_send, b_recv, {"ep": to}).start()
        return carry

    lax.fori_loop(1, PEERS, giveback, 0)
    own = pltpu.make_async_copy(send2.at[me], back.at[me], own_sem.at[1])
    own.start()
    own.wait()
    arrived = remote(
        send2.at[whole], back.at[whole], b_send, b_recv, {"ep": lax.rem(me + 1, PEERS)}
    )
    arrived.wait()

    results = back[...].astype(F32).reshape(PEERS * 8, LANES).astype(BF)
    mixed = jnp.dot(high, results, preferred_element_type=F32) * 256.0
    mixed = mixed + jnp.dot(low, results, preferred_element_type=F32)
    mixed = (mixed / total).astype(BF)
    for i in range(DP):
        outp[i] = mixed[i * 16 : (i + 1) * 16]
    copies = []
    for d in range(1, DP):
        to = lax.rem(q + d, DP)
        copies.append(remote(outp.at[to], fin.at[q], fs.at[d - 1], fr.at[d - 1], {"dp": to}))
        copies[-1].start()
    out_ref[q] = outp[q]
    for d in range(1, DP):
        copies[d - 1].wait()
        src = lax.rem(q + DP - d, DP)
        out_ref[src] = fin[src]


def per_device(tokens, dest_ids, gate_fixed, gate_up, down):
    own = tokens[0].reshape(4, DP, 4, LANES).transpose(1, 0, 2, 3).reshape(DP, 16, LANES)
    gates = gate_fixed[0]
    routes = jnp.concatenate([dest_ids[0], gates >> 8, gates & 255], axis=1)
    routes = jnp.pad(routes, ((0, 0), (0, LANES - 3 * TOP))).astype(BF)
    routes = jnp.broadcast_to(routes[None, :, None, :], (DP, 4, 4, LANES)).reshape(DP, 16, LANES)
    msg = jnp.concatenate([own, routes], axis=1)
    dma = pltpu.SemaphoreType.DMA
    out = pl.pallas_call(
        kernel,
        out_shape=jax.ShapeDtypeStruct((DP, 16, LANES), BF),
        in_specs=[
            pl.BlockSpec(memory_space=pltpu.VMEM),
            pl.BlockSpec(memory_space=pl.ANY),
            pl.BlockSpec(memory_space=pl.ANY),
        ],
        out_specs=pl.BlockSpec(memory_space=pltpu.VMEM),
        scratch_shapes=[
            pltpu.VMEM((DP, 32, LANES), BF),
            pltpu.VMEM(gate_up.shape[1:], BF),
            pltpu.VMEM(down.shape[1:], BF),
            pltpu.VMEM((PEERS, 8, LANES), BF),
            pltpu.VMEM((DP, PEERS, 8, LANES), BF),
            pltpu.VMEM((PEERS * 2, QUARTER), BF),
            pltpu.VMEM((DP, PEERS * 2, QUARTER), BF),
            pltpu.VMEM((DP, PEERS * 2, QUARTER), BF),
            pltpu.VMEM((PEERS, 8, LANES), BF),
            pltpu.VMEM((PEERS, 8, LANES), BF),
            pltpu.VMEM((DP, 16, LANES), BF),
            pltpu.VMEM((DP, 16, LANES), BF),
            dma((2,)), dma((3,)), dma((3,)), dma, dma, dma((3,)), dma((3,)),
            dma((3,)), dma((3,)), dma, dma, dma((3,)), dma((3,)), dma((2,)),
        ],
        compiler_params=pltpu.CompilerParams(collective_id=0, has_side_effects=True),
        name="routed_experts",
    )(msg, gate_up[0], down[0])
    return out.reshape(DP, 4, 4, LANES).transpose(1, 0, 2, 3).reshape(1, 4, DP * QUARTER)


def solution(mesh):
    return jax.shard_map(
        per_device,
        mesh=mesh,
        in_specs=(
            P("ep", "dp", None),
            P("ep", "dp", None),
            P("ep", "dp", None),
            P("ep", None, "dp", None),
            P("ep", "dp", None),
        ),
        out_specs=P("ep", "dp", None),
        check_vma=False,
    )
```

```python
import jax
import jax.numpy as jnp
from jax import lax
from jax.experimental import pallas as pl
from jax.experimental.pallas import tpu as pltpu
from jax.sharding import PartitionSpec as P

BF = jnp.bfloat16
F32 = jnp.float32
MESH = pl.DeviceIdType.MESH
PEERS = 128
DP = 4
TOP = 8
LANES = 128
QUARTER = 512
STRIDE = 43
GROUPS = 2
GROUP = PEERS // GROUPS


def iota(shape, dim):
    return lax.broadcasted_iota(jnp.int32, shape, dim)


def permutation(inverse):
    moved = iota((128, 128), 1 if inverse else 0)
    place = iota((128, 128), 0 if inverse else 1)
    home = (moved & 31) // 2 * 8 + (moved & 1) * 4 + moved // 32
    return jnp.where(home == place, 1.0, 0.0).astype(BF)


def remote(src, dst, send_sem, recv_sem, device):
    return pltpu.make_async_remote_copy(
        src_ref=src, dst_ref=dst, send_sem=send_sem, recv_sem=recv_sem,
        device_id=device, device_id_type=MESH,
    )


def kernel(
    tokens_ref, ids_ref, gates_ref, pair_hbm, lower_hbm, out_ref,
    msg, table_ref, got, pair, lower, send1, recv1, rows, part, pin, send2, back, outp, fin,
    local_sem, xs, xr, a_send, a_recv, gs, gr, rs, rr, b_send, b_recv, fs, fr, own_sem,
):
    q = lax.axis_index("dp")
    me = lax.axis_index("ep")
    load_pair = pltpu.make_async_copy(pair_hbm, pair, local_sem.at[0])
    load_lower = pltpu.make_async_copy(lower_hbm, lower, local_sem.at[1])
    load_pair.start()
    load_lower.start()

    barrier = pltpu.get_barrier_semaphore()
    for d in range(1, DP):
        pl.semaphore_signal(
            barrier, inc=1, device_id={"dp": lax.rem(q + d, DP)}, device_id_type=MESH
        )

    def greet(d, carry):
        pl.semaphore_signal(
            barrier, inc=1, device_id={"ep": lax.rem(me + d, PEERS)}, device_id_type=MESH
        )
        return carry

    lax.fori_loop(1, PEERS, greet, 0)

    table_ref[...] = jnp.zeros(table_ref.shape, F32)
    table_ref[:, 0:TOP] = ids_ref[...].astype(F32)
    table_ref[:, TOP : 2 * TOP] = (gates_ref[...] >> 8).astype(F32)
    table_ref[:, 2 * TOP : 3 * TOP] = (gates_ref[...] & 255).astype(F32)
    routes = jnp.concatenate([table_ref[...]] * 4, axis=0).astype(BF)
    for i in range(DP):
        pieces = [
            tokens_ref[:, i * QUARTER + j * LANES : i * QUARTER + (j + 1) * LANES].astype(F32)
            for j in range(4)
        ]
        msg[i, 0:16] = jnp.concatenate(pieces, axis=0).astype(BF)
        msg[i, 16:32] = routes
    pl.semaphore_wait(barrier, DP - 1 + PEERS - 1)
    copies = []
    for d in range(1, DP):
        to = lax.rem(q + d, DP)
        copies.append(
            remote(msg.at[to], got.at[q], xs.at[d - 1], xr.at[d - 1], {"dp": to})
        )
        copies[-1].start()
    got[q] = msg[q]
    for copy in copies:
        copy.wait()

    tok = jnp.concatenate([got[i, 0:16, :] for i in range(DP)], axis=0)
    table = jnp.concatenate([got[i, 16:32, :].astype(F32) for i in range(DP)], axis=0)
    wide = (64, PEERS * 8)
    column = iota(wide, 1)
    expert = (column // 8).astype(F32)
    named = jnp.zeros(wide, F32)
    high = jnp.zeros(wide, F32)
    low = jnp.zeros(wide, F32)
    total = jnp.zeros((64, 1), F32)
    for k in range(TOP):
        same = table[:, k : k + 1] == expert
        hi, lo = table[:, TOP + k : TOP + k + 1], table[:, 2 * TOP + k : 2 * TOP + k + 1]
        total = total + (hi * 256.0 + lo)
        named = jnp.where(same, 1.0, named)
        high = jnp.where(same, hi, high)
        low = jnp.where(same, lo, low)
    line, other = iota((64, 64), 0), iota((64, 64), 1)
    before = other // 16 * 4 + (other & 3) < line // 16 * 4 + (line & 3)
    earlier = jnp.where(before & ((other // 4 & 3) == 0), 1.0, 0.0).astype(BF)
    rank = jnp.dot(earlier, named.astype(BF), preferred_element_type=F32)
    slot = ((column // 4) & 1).astype(F32)
    live = (rank == slot) & ((iota(wide, 0) // 4 & 3) == (column & 3))
    pick = jnp.where(live, named, 0.0)
    high = jnp.where(live, high, 0.0).astype(BF)
    low = jnp.where(live, low, 0.0).astype(BF)
    packed = jnp.dot(pick.T.astype(BF), tok, preferred_element_type=F32)
    send1[...] = packed.reshape(PEERS, 8, LANES).astype(BF)

    for g in range(GROUPS):

        def dispatch(i, carry):
            to = lax.rem(me + i * STRIDE, PEERS)
            remote(send1.at[to], recv1.at[q, i], a_send.at[g], a_recv.at[g], {"ep": to}).start()
            return carry

        lax.fori_loop(max(1, g * GROUP), (g + 1) * GROUP, dispatch, 0)
    own = pltpu.make_async_copy(send1.at[me], recv1.at[q, 0], own_sem.at[0])
    own.start()
    own.wait()

    gathers = {}
    for g in range(GROUPS):
        first = max(1, g * GROUP)
        span = pl.ds(first, (g + 1) * GROUP - first)
        remote(
            send1.at[span], recv1.at[q, span], a_send.at[g], a_recv.at[g],
            {"ep": lax.rem(me + 1, PEERS)},
        ).wait()
        span = pl.ds(g * GROUP, GROUP)
        for d in (2, 1, 3):
            to = lax.rem(q + d, DP)
            gathers[g, d] = remote(
                recv1.at[q, span], recv1.at[q, span], gs.at[d - 1, g], gr.at[d - 1, g], {"dp": to}
            )
            gathers[g, d].start()
    load_pair.wait()
    load_lower.wait()
    order = permutation(False)
    back_order = permutation(True)
    contract = (((1,), (1,)), ((), ()))
    reduces = {}

    def experts(g):
        gate = jnp.zeros((GROUP * 2, pair.shape[1]), F32)
        upper = jnp.zeros((GROUP * 2, pair.shape[1]), F32)
        for d in (0, 1, 3, 2):
            if d:
                gathers[g, d].wait()
            src = lax.rem(q + DP - d, DP)
            for b in range(GROUP // 16):
                start = g * GROUP + b * 16
                block = recv1[src, start : start + 16].astype(F32).reshape(128, LANES).astype(BF)
                moved = jnp.dot(order, block, preferred_element_type=F32).astype(BF)
                for j in range(4):
                    rows[g, b * 32 : (b + 1) * 32, j * LANES : (j + 1) * LANES] = moved[
                        j * 32 : (j + 1) * 32
                    ]
            x = rows[g]
            features = pl.ds(pl.multiple_of(src * QUARTER, QUARTER), QUARTER)
            gate = gate + lax.dot_general(
                x, pair[0, :, features], contract, preferred_element_type=F32
            )
            upper = upper + lax.dot_general(
                x, pair[1, :, features], contract, preferred_element_type=F32
            )
        hidden = (gate / (1.0 + jnp.exp(-gate)) * upper).astype(BF)
        for d in (2, 1, 3, 0):
            to = lax.rem(q + d, DP)
            features = pl.ds(pl.multiple_of(to * QUARTER, QUARTER), QUARTER)
            part[g, to] = jnp.dot(hidden, lower[:, features], preferred_element_type=F32).astype(BF)
            if d:
                reduces[g, d] = remote(
                    part.at[g, to], pin.at[g, q], rs.at[d - 1, g], rr.at[d - 1, g], {"dp": to}
                )
                reduces[g, d].start()

    def finish(g):
        for d in (1, 3, 2):
            reduces[g, d].wait()
        for b in range(GROUP // 16):
            lines = slice(b * 32, (b + 1) * 32)
            added = part[g, q, lines].astype(F32)
            for d in range(1, DP):
                added = added + pin[g, lax.rem(q + DP - d, DP), lines].astype(F32)
            added = added.astype(BF)
            stacked = jnp.concatenate(
                [added[:, j * LANES : (j + 1) * LANES] for j in range(4)], axis=0
            )
            moved = jnp.dot(back_order, stacked, preferred_element_type=F32)
            start = g * GROUP + b * 16
            send2[start : start + 16] = moved.reshape(16, 8, LANES).astype(BF)

        def giveback(i, carry):
            to = lax.rem(me + i * (PEERS - STRIDE), PEERS)
            remote(send2.at[i], back.at[me], b_send, b_recv, {"ep": to}).start()
            return carry

        lax.fori_loop(max(1, g * GROUP), (g + 1) * GROUP, giveback, 0)

    for g in range(GROUPS):
        experts(g)
        if g:
            finish(g - 1)
    finish(GROUPS - 1)
    own = pltpu.make_async_copy(send2.at[0], back.at[me], own_sem.at[1])
    own.start()
    own.wait()
    whole = pl.ds(0, PEERS - 1)
    remote(
        send2.at[whole], back.at[whole], b_send, b_recv, {"ep": lax.rem(me + 1, PEERS)}
    ).wait()

    results = back[...].astype(F32).reshape(PEERS * 8, LANES).astype(BF)
    mixed = jnp.dot(high, results, preferred_element_type=F32) * 256.0
    mixed = mixed + jnp.dot(low, results, preferred_element_type=F32)
    mixed = (mixed / total).astype(BF)
    for i in range(DP):
        outp[i] = mixed[i * 16 : (i + 1) * 16]
    copies = []
    for d in range(1, DP):
        to = lax.rem(q + d, DP)
        copies.append(remote(outp.at[to], fin.at[q], fs.at[d - 1], fr.at[d - 1], {"dp": to}))
        copies[-1].start()
    for d in range(DP):
        if d:
            copies[d - 1].wait()
        src = lax.rem(q + DP - d, DP)
        value = (fin[src] if d else outp[q]).astype(F32)
        for j in range(4):
            features = pl.ds(pl.multiple_of(src * QUARTER + j * LANES, LANES), LANES)
            out_ref[:, features] = value[j * 4 : (j + 1) * 4].astype(BF)


def per_device(tokens, dest_ids, gate_fixed, gate_up, down):
    dma = pltpu.SemaphoreType.DMA
    out = pl.pallas_call(
        kernel,
        out_shape=jax.ShapeDtypeStruct((4, DP * QUARTER), BF),
        in_specs=[
            pl.BlockSpec(memory_space=pltpu.VMEM),
            pl.BlockSpec(memory_space=pltpu.VMEM),
            pl.BlockSpec(memory_space=pltpu.VMEM),
            pl.BlockSpec(memory_space=pl.ANY),
            pl.BlockSpec(memory_space=pl.ANY),
        ],
        out_specs=pl.BlockSpec(memory_space=pltpu.VMEM),
        scratch_shapes=[
            pltpu.VMEM((DP, 32, LANES), BF),
            pltpu.VMEM((4, LANES), F32),
            pltpu.VMEM((DP, 32, LANES), BF),
            pltpu.VMEM(gate_up.shape[1:], BF),
            pltpu.VMEM(down.shape[1:], BF),
            pltpu.VMEM((PEERS, 8, LANES), BF),
            pltpu.VMEM((DP, PEERS, 8, LANES), BF),
            pltpu.VMEM((GROUPS, GROUP * 2, QUARTER), BF),
            pltpu.VMEM((GROUPS, DP, GROUP * 2, QUARTER), BF),
            pltpu.VMEM((GROUPS, DP, GROUP * 2, QUARTER), BF),
            pltpu.VMEM((PEERS, 8, LANES), BF),
            pltpu.VMEM((PEERS, 8, LANES), BF),
            pltpu.VMEM((DP, 16, LANES), BF),
            pltpu.VMEM((DP, 16, LANES), BF),
            dma((2,)), dma((3,)), dma((3,)), dma((GROUPS,)), dma((GROUPS,)),
            dma((3, GROUPS)), dma((3, GROUPS)), dma((3, GROUPS)), dma((3, GROUPS)),
            dma, dma, dma((3,)), dma((3,)), dma((2,)),
        ],
        compiler_params=pltpu.CompilerParams(collective_id=0, has_side_effects=True),
        name="routed_experts",
    )(tokens[0], dest_ids[0], gate_fixed[0], gate_up[0], down[0])
    return out[None]


def solution(mesh):
    return jax.shard_map(
        per_device,
        mesh=mesh,
        in_specs=(
            P("ep", "dp", None),
            P("ep", "dp", None),
            P("ep", "dp", None),
            P("ep", None, "dp", None),
            P("ep", "dp", None),
        ),
        out_specs=P("ep", "dp", None),
        check_vma=False,
    )
```

```python
import jax
import jax.numpy as jnp
from jax import lax
from jax.experimental import pallas as pl
from jax.experimental.pallas import tpu as pltpu
from jax.sharding import PartitionSpec as P

BF = jnp.bfloat16
F32 = jnp.float32
MESH = pl.DeviceIdType.MESH
PEERS = 128
DP = 4
TOP = 8
LANES = 128
QUARTER = 512
STRIDE = 43
GROUPS = 4
GROUP = PEERS // GROUPS


def iota(shape, dim):
    return lax.broadcasted_iota(jnp.int32, shape, dim)


def permutation(inverse):
    moved = iota((128, 128), 1 if inverse else 0)
    place = iota((128, 128), 0 if inverse else 1)
    home = (moved & 31) // 2 * 8 + (moved & 1) * 4 + moved // 32
    return jnp.where(home == place, 1.0, 0.0).astype(BF)


def remote(src, dst, send_sem, recv_sem, device):
    return pltpu.make_async_remote_copy(
        src_ref=src, dst_ref=dst, send_sem=send_sem, recv_sem=recv_sem,
        device_id=device, device_id_type=MESH,
    )


def kernel(
    tokens_ref, ids_ref, gates_ref, pair_hbm, lower_hbm, out_ref,
    msg, table_ref, got, pair, lower, send1, recv1, rows, part, pin, send2, back, outp, fin,
    local_sem, xs, xr, a_send, a_recv, gs, gr, rs, rr, b_send, b_recv, fs, fr, own_sem, line_sem, twin_sem,
):
    q = lax.axis_index("dp")
    me = lax.axis_index("ep")
    load_pair = pltpu.make_async_copy(pair_hbm, pair, local_sem.at[0])
    load_lower = pltpu.make_async_copy(lower_hbm, lower, local_sem.at[1])
    load_pair.start()
    load_lower.start()

    barrier = pltpu.get_barrier_semaphore()
    for d in range(1, DP):
        pl.semaphore_signal(
            barrier, inc=1, device_id={"dp": lax.rem(q + d, DP)}, device_id_type=MESH
        )

    z, y, core = me // 16, me // 2 % 8, me % 2
    line = [lax.rem(me + 16 * d, PEERS) for d in range(1, 8)]
    across = [z * 16 + lax.rem(y + d, 8) * 2 + core for d in range(1, 8)]
    twin = z * 16 + y * 2 + (1 - core)
    for to in line + across + [twin]:
        pl.semaphore_signal(barrier, inc=1, device_id={"ep": to}, device_id_type=MESH)

    table_ref[...] = jnp.zeros(table_ref.shape, F32)
    table_ref[:, 0:TOP] = ids_ref[...].astype(F32)
    table_ref[:, TOP : 2 * TOP] = (gates_ref[...] >> 8).astype(F32)
    table_ref[:, 2 * TOP : 3 * TOP] = (gates_ref[...] & 255).astype(F32)
    routes = jnp.concatenate([table_ref[...]] * 4, axis=0).astype(BF)
    for i in range(DP):
        pieces = [
            tokens_ref[:, i * QUARTER + j * LANES : i * QUARTER + (j + 1) * LANES].astype(F32)
            for j in range(4)
        ]
        msg[i, 0:16] = jnp.concatenate(pieces, axis=0).astype(BF)
        msg[i, 16:32] = routes
    pl.semaphore_wait(barrier, DP - 1 + 15)
    for to in line:
        pl.semaphore_signal(line_sem, inc=1, device_id={"ep": to}, device_id_type=MESH)
    copies = []
    for d in range(1, DP):
        to = lax.rem(q + d, DP)
        copies.append(
            remote(msg.at[to], got.at[q], xs.at[d - 1], xr.at[d - 1], {"dp": to})
        )
        copies[-1].start()
    got[q] = msg[q]
    pl.semaphore_wait(line_sem, 7)
    pl.semaphore_signal(twin_sem, inc=1, device_id={"ep": twin}, device_id_type=MESH)
    for copy in copies:
        copy.wait()

    tok = jnp.concatenate([got[i, 0:16, :] for i in range(DP)], axis=0)
    table = jnp.concatenate([got[i, 16:32, :].astype(F32) for i in range(DP)], axis=0)
    wide = (64, PEERS * 8)
    column = iota(wide, 1)
    expert = (column // 8).astype(F32)
    named = jnp.zeros(wide, F32)
    high = jnp.zeros(wide, F32)
    low = jnp.zeros(wide, F32)
    total = jnp.zeros((64, 1), F32)
    for k in range(TOP):
        same = table[:, k : k + 1] == expert
        hi, lo = table[:, TOP + k : TOP + k + 1], table[:, 2 * TOP + k : 2 * TOP + k + 1]
        total = total + (hi * 256.0 + lo)
        named = jnp.where(same, 1.0, named)
        high = jnp.where(same, hi, high)
        low = jnp.where(same, lo, low)
    this, other = iota((64, 64), 0), iota((64, 64), 1)
    before = other // 16 * 4 + (other & 3) < this // 16 * 4 + (this & 3)
    earlier = jnp.where(before & ((other // 4 & 3) == 0), 1.0, 0.0).astype(BF)
    rank = jnp.dot(earlier, named.astype(BF), preferred_element_type=F32)
    slot = ((column // 4) & 1).astype(F32)
    live = (rank == slot) & ((iota(wide, 0) // 4 & 3) == (column & 3))
    pick = jnp.where(live, named, 0.0)
    high = jnp.where(live, high, 0.0).astype(BF)
    low = jnp.where(live, low, 0.0).astype(BF)
    packed = jnp.dot(pick.T.astype(BF), tok, preferred_element_type=F32)
    send1[...] = packed.reshape(PEERS, 8, LANES).astype(BF)

    pl.semaphore_wait(twin_sem, 1)

    for g in range(GROUPS):

        def dispatch(i, carry):
            to = lax.rem(me + i * STRIDE, PEERS)
            remote(send1.at[to], recv1.at[q, i], a_send.at[g], a_recv.at[g], {"ep": to}).start()
            return carry

        lax.fori_loop(max(1, g * GROUP), (g + 1) * GROUP, dispatch, 0)
    own = pltpu.make_async_copy(send1.at[me], recv1.at[q, 0], own_sem.at[0])
    own.start()
    own.wait()

    gathers = {}
    for g in range(GROUPS):
        first = max(1, g * GROUP)
        span = pl.ds(first, (g + 1) * GROUP - first)
        remote(
            send1.at[span], recv1.at[q, span], a_send.at[g], a_recv.at[g],
            {"ep": lax.rem(me + 1, PEERS)},
        ).wait()
        span = pl.ds(g * GROUP, GROUP)
        for d in (2, 1, 3):
            to = lax.rem(q + d, DP)
            gathers[g, d] = remote(
                recv1.at[q, span], recv1.at[q, span], gs.at[d - 1, g], gr.at[d - 1, g], {"dp": to}
            )
            gathers[g, d].start()
    load_pair.wait()
    load_lower.wait()
    order = permutation(False)
    back_order = permutation(True)
    contract = (((1,), (1,)), ((), ()))
    reduces = {}

    def experts(g):
        gate = jnp.zeros((GROUP * 2, pair.shape[1]), F32)
        upper = jnp.zeros((GROUP * 2, pair.shape[1]), F32)
        for d in (0, 1, 3, 2):
            if d:
                gathers[g, d].wait()
            src = lax.rem(q + DP - d, DP)
            for b in range(GROUP // 16):
                start = g * GROUP + b * 16
                block = recv1[src, start : start + 16].astype(F32).reshape(128, LANES).astype(BF)
                moved = jnp.dot(order, block, preferred_element_type=F32).astype(BF)
                for j in range(4):
                    rows[g, b * 32 : (b + 1) * 32, j * LANES : (j + 1) * LANES] = moved[
                        j * 32 : (j + 1) * 32
                    ]
            x = rows[g]
            features = pl.ds(pl.multiple_of(src * QUARTER, QUARTER), QUARTER)
            gate = gate + lax.dot_general(
                x, pair[0, :, features], contract, preferred_element_type=F32
            )
            upper = upper + lax.dot_general(
                x, pair[1, :, features], contract, preferred_element_type=F32
            )
        hidden = (gate / (1.0 + jnp.exp(-gate)) * upper).astype(BF)
        for d in (2, 1, 3, 0):
            to = lax.rem(q + d, DP)
            features = pl.ds(pl.multiple_of(to * QUARTER, QUARTER), QUARTER)
            part[g, to] = jnp.dot(hidden, lower[:, features], preferred_element_type=F32).astype(BF)
            if d:
                reduces[g, d] = remote(
                    part.at[g, to], pin.at[g, q], rs.at[d - 1, g], rr.at[d - 1, g], {"dp": to}
                )
                reduces[g, d].start()

    def finish(g):
        for d in (1, 3, 2):
            reduces[g, d].wait()
        for b in range(GROUP // 16):
            lines = slice(b * 32, (b + 1) * 32)
            added = part[g, q, lines].astype(F32)
            for d in range(1, DP):
                added = added + pin[g, lax.rem(q + DP - d, DP), lines].astype(F32)
            added = added.astype(BF)
            stacked = jnp.concatenate(
                [added[:, j * LANES : (j + 1) * LANES] for j in range(4)], axis=0
            )
            moved = jnp.dot(back_order, stacked, preferred_element_type=F32)
            start = g * GROUP + b * 16
            send2[start : start + 16] = moved.reshape(16, 8, LANES).astype(BF)

        def giveback(i, carry):
            to = lax.rem(me + i * (PEERS - STRIDE), PEERS)
            remote(send2.at[i], back.at[me], b_send, b_recv, {"ep": to}).start()
            return carry

        lax.fori_loop(max(1, g * GROUP), (g + 1) * GROUP, giveback, 0)

    for g in range(GROUPS):
        experts(g)
        if g:
            finish(g - 1)
    finish(GROUPS - 1)
    own = pltpu.make_async_copy(send2.at[0], back.at[me], own_sem.at[1])
    own.start()
    own.wait()
    whole = pl.ds(0, PEERS - 1)
    remote(
        send2.at[whole], back.at[whole], b_send, b_recv, {"ep": lax.rem(me + 1, PEERS)}
    ).wait()

    results = back[...].astype(F32).reshape(PEERS * 8, LANES).astype(BF)
    mixed = jnp.dot(high, results, preferred_element_type=F32) * 256.0
    mixed = mixed + jnp.dot(low, results, preferred_element_type=F32)
    mixed = (mixed / total).astype(BF)
    for i in range(DP):
        outp[i] = mixed[i * 16 : (i + 1) * 16]
    copies = []
    for d in range(1, DP):
        to = lax.rem(q + d, DP)
        copies.append(remote(outp.at[to], fin.at[q], fs.at[d - 1], fr.at[d - 1], {"dp": to}))
        copies[-1].start()
    for d in range(DP):
        if d:
            copies[d - 1].wait()
        src = lax.rem(q + DP - d, DP)
        value = (fin[src] if d else outp[q]).astype(F32)
        for j in range(4):
            features = pl.ds(pl.multiple_of(src * QUARTER + j * LANES, LANES), LANES)
            out_ref[:, features] = value[j * 4 : (j + 1) * 4].astype(BF)


def per_device(tokens, dest_ids, gate_fixed, gate_up, down):
    dma = pltpu.SemaphoreType.DMA
    out = pl.pallas_call(
        kernel,
        out_shape=jax.ShapeDtypeStruct((4, DP * QUARTER), BF),
        in_specs=[
            pl.BlockSpec(memory_space=pltpu.VMEM),
            pl.BlockSpec(memory_space=pltpu.VMEM),
            pl.BlockSpec(memory_space=pltpu.VMEM),
            pl.BlockSpec(memory_space=pl.ANY),
            pl.BlockSpec(memory_space=pl.ANY),
        ],
        out_specs=pl.BlockSpec(memory_space=pltpu.VMEM),
        scratch_shapes=[
            pltpu.VMEM((DP, 32, LANES), BF),
            pltpu.VMEM((4, LANES), F32),
            pltpu.VMEM((DP, 32, LANES), BF),
            pltpu.VMEM(gate_up.shape[1:], BF),
            pltpu.VMEM(down.shape[1:], BF),
            pltpu.VMEM((PEERS, 8, LANES), BF),
            pltpu.VMEM((DP, PEERS, 8, LANES), BF),
            pltpu.VMEM((GROUPS, GROUP * 2, QUARTER), BF),
            pltpu.VMEM((GROUPS, DP, GROUP * 2, QUARTER), BF),
            pltpu.VMEM((GROUPS, DP, GROUP * 2, QUARTER), BF),
            pltpu.VMEM((PEERS, 8, LANES), BF),
            pltpu.VMEM((PEERS, 8, LANES), BF),
            pltpu.VMEM((DP, 16, LANES), BF),
            pltpu.VMEM((DP, 16, LANES), BF),
            dma((2,)), dma((3,)), dma((3,)), dma((GROUPS,)), dma((GROUPS,)),
            dma((3, GROUPS)), dma((3, GROUPS)), dma((3, GROUPS)), dma((3, GROUPS)),
            dma, dma, dma((3,)), dma((3,)), dma((2,)),
            pltpu.SemaphoreType.REGULAR, pltpu.SemaphoreType.REGULAR,
        ],
        compiler_params=pltpu.CompilerParams(collective_id=0, has_side_effects=True),
        name="routed_experts",
    )(tokens[0], dest_ids[0], gate_fixed[0], gate_up[0], down[0])
    return out[None]


def solution(mesh):
    return jax.shard_map(
        per_device,
        mesh=mesh,
        in_specs=(
            P("ep", "dp", None),
            P("ep", "dp", None),
            P("ep", "dp", None),
            P("ep", None, "dp", None),
            P("ep", "dp", None),
        ),
        out_specs=P("ep", "dp", None),
        check_vma=False,
    )
```

```python
import jax
import jax.numpy as jnp
from jax import lax
from jax.experimental import pallas as pl
from jax.experimental.pallas import tpu as pltpu
from jax.sharding import PartitionSpec as P

BF = jnp.bfloat16
F32 = jnp.float32
MESH = pl.DeviceIdType.MESH
PEERS = 128
DP = 4
TOP = 8
LANES = 128
QUARTER = 512
STRIDE = 43
GROUPS = 2
GROUP = PEERS // GROUPS


def iota(shape, dim):
    return lax.broadcasted_iota(jnp.int32, shape, dim)


def permutation(inverse):
    moved = iota((128, 128), 1 if inverse else 0)
    place = iota((128, 128), 0 if inverse else 1)
    home = (moved & 31) // 2 * 8 + (moved & 1) * 4 + moved // 32
    return jnp.where(home == place, 1.0, 0.0).astype(BF)


def remote(src, dst, send_sem, recv_sem, device):
    return pltpu.make_async_remote_copy(
        src_ref=src, dst_ref=dst, send_sem=send_sem, recv_sem=recv_sem,
        device_id=device, device_id_type=MESH,
    )


def kernel(
    tokens_ref, ids_ref, gates_ref, pair_hbm, lower_hbm, out_ref,
    msg, table_ref, got, pair, lower, send1, recv1, rows, part, pin, send2, back, outp, fin,
    local_sem, xs, xr, a_send, a_recv, gs, gr, rs, rr, b_send, b_recv, fs, fr, own_sem, line_sem, twin_sem, hs, hr,
    hop, us, ur, ws, wr,
):
    q = lax.axis_index("dp")
    me = lax.axis_index("ep")
    load_pair = pltpu.make_async_copy(pair_hbm, pair, local_sem.at[0])
    load_lower = pltpu.make_async_copy(lower_hbm, lower, local_sem.at[1])
    load_pair.start()
    load_lower.start()

    barrier = pltpu.get_barrier_semaphore()
    for d in range(1, DP):
        pl.semaphore_signal(
            barrier, inc=1, device_id={"dp": lax.rem(q + d, DP)}, device_id_type=MESH
        )

    z, y, core = me // 16, me // 2 % 8, me % 2
    line = [lax.rem(me + 16 * d, PEERS) for d in range(1, 8)]
    across = [z * 16 + lax.rem(y + d, 8) * 2 + core for d in range(1, 8)]
    twin = z * 16 + y * 2 + (1 - core)
    for to in line + across + [twin]:
        pl.semaphore_signal(barrier, inc=1, device_id={"ep": to}, device_id_type=MESH)

    table_ref[...] = jnp.zeros(table_ref.shape, F32)
    table_ref[:, 0:TOP] = ids_ref[...].astype(F32)
    table_ref[:, TOP : 2 * TOP] = (gates_ref[...] >> 8).astype(F32)
    table_ref[:, 2 * TOP : 3 * TOP] = (gates_ref[...] & 255).astype(F32)
    routes = jnp.concatenate([table_ref[...]] * 4, axis=0).astype(BF)
    for i in range(DP):
        pieces = [
            tokens_ref[:, i * QUARTER + j * LANES : i * QUARTER + (j + 1) * LANES].astype(F32)
            for j in range(4)
        ]
        msg[i, 0:16] = jnp.concatenate(pieces, axis=0).astype(BF)
        msg[i, 16:32] = routes
    pl.semaphore_wait(barrier, DP - 1 + 15)
    for to in line:
        pl.semaphore_signal(line_sem, inc=1, device_id={"ep": to}, device_id_type=MESH)
    copies = []
    for d in range(1, DP):
        to = lax.rem(q + d, DP)
        copies.append(
            remote(msg.at[to], got.at[q], xs.at[d - 1], xr.at[d - 1], {"dp": to})
        )
        copies[-1].start()
    got[q] = msg[q]
    pl.semaphore_wait(line_sem, 7)
    pl.semaphore_signal(twin_sem, inc=1, device_id={"ep": twin}, device_id_type=MESH)
    for copy in copies:
        copy.wait()

    tok = jnp.concatenate([got[i, 0:16, :] for i in range(DP)], axis=0)
    table = jnp.concatenate([got[i, 16:32, :].astype(F32) for i in range(DP)], axis=0)
    wide = (64, PEERS * 8)
    column = iota(wide, 1)
    expert = (column // 8).astype(F32)
    named = jnp.zeros(wide, F32)
    high = jnp.zeros(wide, F32)
    low = jnp.zeros(wide, F32)
    total = jnp.zeros((64, 1), F32)
    for k in range(TOP):
        same = table[:, k : k + 1] == expert
        hi, lo = table[:, TOP + k : TOP + k + 1], table[:, 2 * TOP + k : 2 * TOP + k + 1]
        total = total + (hi * 256.0 + lo)
        named = jnp.where(same, 1.0, named)
        high = jnp.where(same, hi, high)
        low = jnp.where(same, lo, low)
    this, other = iota((64, 64), 0), iota((64, 64), 1)
    before = other // 16 * 4 + (other & 3) < this // 16 * 4 + (this & 3)
    earlier = jnp.where(before & ((other // 4 & 3) == 0), 1.0, 0.0).astype(BF)
    rank = jnp.dot(earlier, named.astype(BF), preferred_element_type=F32)
    slot = ((column // 4) & 1).astype(F32)
    live = (rank == slot) & ((iota(wide, 0) // 4 & 3) == (column & 3))
    pick = jnp.where(live, named, 0.0)
    high = jnp.where(live, high, 0.0).astype(BF)
    low = jnp.where(live, low, 0.0).astype(BF)
    packed = jnp.dot(pick.T.astype(BF), tok, preferred_element_type=F32)
    send1[...] = packed.reshape(PEERS, 8, LANES).astype(BF)

    pl.semaphore_wait(twin_sem, 1)

    for g in range(GROUPS):

        def dispatch(i, carry):
            to = lax.rem(me + i * STRIDE, PEERS)
            remote(send1.at[to], recv1.at[q, i], a_send.at[g], a_recv.at[g], {"ep": to}).start()
            return carry

        lax.fori_loop(max(1, g * GROUP), (g + 1) * GROUP, dispatch, 0)
    own = pltpu.make_async_copy(send1.at[me], recv1.at[q, 0], own_sem.at[0])
    own.start()
    own.wait()

    gathers = {}
    relays = {}
    half = GROUP // 2

    def relay(g):
        for d in (1, 3):
            gathers[g, d].wait_recv()
            src = lax.rem(q + DP - d, DP)
            span = pl.ds(g * GROUP + (0 if d == 1 else half), half)
            relays[g, d] = remote(
                recv1.at[src, span], recv1.at[src, span], hs.at[d // 2, g], hr.at[d // 2, g],
                {"dp": lax.rem(q + d, DP)},
            )
            relays[g, d].start()

    for g in range(GROUPS):
        first = max(1, g * GROUP)
        span = pl.ds(first, (g + 1) * GROUP - first)
        remote(
            send1.at[span], recv1.at[q, span], a_send.at[g], a_recv.at[g],
            {"ep": lax.rem(me + 1, PEERS)},
        ).wait()
        span = pl.ds(g * GROUP, GROUP)
        for d in (1, 3):
            to = lax.rem(q + d, DP)
            gathers[g, d] = remote(
                recv1.at[q, span], recv1.at[q, span], gs.at[d - 1, g], gr.at[d - 1, g], {"dp": to}
            )
            gathers[g, d].start()
        if g:
            relay(g - 1)
    load_pair.wait()
    load_lower.wait()
    order = permutation(False)
    back_order = permutation(True)
    contract = (((1,), (1,)), ((), ()))
    reduces, hops, sums = {}, {}, {}
    first_half, second_half = pl.ds(0, GROUP), pl.ds(GROUP, GROUP)

    def experts(g):
        gate = jnp.zeros((GROUP * 2, pair.shape[1]), F32)
        upper = jnp.zeros((GROUP * 2, pair.shape[1]), F32)
        for d in (0, 1, 3, 2):
            if g == 0 and d == 1:
                relay(GROUPS - 1)
            if d == 2:
                for copy in (relays[g, 1], relays[g, 3]):
                    copy.wait()
            elif d:
                gathers[g, d].wait_send()
            src = lax.rem(q + DP - d, DP)
            blocks = []
            for b in range(GROUP // 16):
                start = g * GROUP + b * 16
                block = recv1[src, start : start + 16].astype(F32).reshape(128, LANES)
                blocks.append(block.astype(BF))
            moved = jnp.dot(
                order, jnp.concatenate(blocks, axis=1), preferred_element_type=F32
            ).astype(BF)
            for b in range(GROUP // 16):
                for j in range(4):
                    rows[g, b * 32 : (b + 1) * 32, j * LANES : (j + 1) * LANES] = moved[
                        j * 32 : (j + 1) * 32, b * LANES : (b + 1) * LANES
                    ]
            x = rows[g]
            features = pl.ds(pl.multiple_of(src * QUARTER, QUARTER), QUARTER)
            gate = gate + lax.dot_general(
                x, pair[0, :, features], contract, preferred_element_type=F32
            )
            upper = upper + lax.dot_general(
                x, pair[1, :, features], contract, preferred_element_type=F32
            )
        if g:
            relay_sum(g - 1)
        hidden = (gate / (1.0 + jnp.exp(-gate)) * upper).astype(BF)
        for d in (2, 1, 3, 0):
            to = lax.rem(q + d, DP)
            features = pl.ds(pl.multiple_of(to * QUARTER, QUARTER), QUARTER)
            part[g, to] = jnp.dot(hidden, lower[:, features], preferred_element_type=F32).astype(BF)
            for side in (1, 3):
                if d == 2:
                    lines = first_half if side == 1 else second_half
                    hops[g, side] = remote(
                        part.at[g, to, lines], hop.at[g, side // 2],
                        us.at[side // 2, g], ur.at[side // 2, g], {"dp": lax.rem(q + side, DP)},
                    )
                    hops[g, side].start()
                elif d == side:
                    lines = second_half if side == 1 else first_half
                    reduces[g, d] = remote(
                        part.at[g, to, lines], pin.at[g, q, lines],
                        rs.at[d - 1, g], rr.at[d - 1, g], {"dp": to},
                    )
                    reduces[g, d].start()

    def relay_sum(g):
        for d in (1, 3):
            hops[g, d].wait()
            to = lax.rem(q + d, DP)
            lines = first_half if d == 1 else second_half
            both = part[g, to, lines].astype(F32) + hop[g, d // 2].astype(F32)
            part[g, to, lines] = both.astype(BF)
            sums[g, d] = remote(
                part.at[g, to, lines], pin.at[g, q, lines],
                ws.at[d // 2, g], wr.at[d // 2, g], {"dp": to},
            )
            sums[g, d].start()

    def finish(g):
        for d in (1, 3):
            reduces[g, d].wait()
            sums[g, d].wait()
        blocks = []
        for b in range(GROUP // 16):
            lines = slice(b * 32, (b + 1) * 32)
            added = part[g, q, lines].astype(F32)
            for d in (1, 3):
                added = added + pin[g, lax.rem(q + DP - d, DP), lines].astype(F32)
            added = added.astype(BF)
            blocks.append(
                jnp.concatenate([added[:, j * LANES : (j + 1) * LANES] for j in range(4)], axis=0)
            )
        moved = jnp.dot(
            back_order, jnp.concatenate(blocks, axis=1), preferred_element_type=F32
        )
        for b in range(GROUP // 16):
            start = g * GROUP + b * 16
            block = moved[:, b * LANES : (b + 1) * LANES]
            send2[start : start + 16] = block.reshape(16, 8, LANES).astype(BF)

        def giveback(i, carry):
            to = lax.rem(me + i * (PEERS - STRIDE), PEERS)
            remote(send2.at[i], back.at[me], b_send, b_recv, {"ep": to}).start()
            return carry

        lax.fori_loop(max(1, g * GROUP), (g + 1) * GROUP, giveback, 0)

    for g in range(GROUPS):
        experts(g)
        if g:
            finish(g - 1)
    relay_sum(GROUPS - 1)
    finish(GROUPS - 1)
    own = pltpu.make_async_copy(send2.at[0], back.at[me], own_sem.at[1])
    own.start()
    own.wait()
    whole = pl.ds(0, PEERS - 1)
    remote(
        send2.at[whole], back.at[whole], b_send, b_recv, {"ep": lax.rem(me + 1, PEERS)}
    ).wait()

    results = back[...].astype(F32).reshape(PEERS * 8, LANES).astype(BF)
    mixed = jnp.dot(high, results, preferred_element_type=F32) * 256.0
    mixed = mixed + jnp.dot(low, results, preferred_element_type=F32)
    mixed = (mixed / total).astype(BF)
    for i in range(DP):
        outp[i] = mixed[i * 16 : (i + 1) * 16]
    copies = []
    for d in range(1, DP):
        to = lax.rem(q + d, DP)
        copies.append(remote(outp.at[to], fin.at[q], fs.at[d - 1], fr.at[d - 1], {"dp": to}))
        copies[-1].start()
    for d in range(DP):
        if d:
            copies[d - 1].wait()
        src = lax.rem(q + DP - d, DP)
        value = (fin[src] if d else outp[q]).astype(F32)
        for j in range(4):
            features = pl.ds(pl.multiple_of(src * QUARTER + j * LANES, LANES), LANES)
            out_ref[:, features] = value[j * 4 : (j + 1) * 4].astype(BF)


def per_device(tokens, dest_ids, gate_fixed, gate_up, down):
    dma = pltpu.SemaphoreType.DMA
    out = pl.pallas_call(
        kernel,
        out_shape=jax.ShapeDtypeStruct((4, DP * QUARTER), BF),
        in_specs=[
            pl.BlockSpec(memory_space=pltpu.VMEM),
            pl.BlockSpec(memory_space=pltpu.VMEM),
            pl.BlockSpec(memory_space=pltpu.VMEM),
            pl.BlockSpec(memory_space=pl.ANY),
            pl.BlockSpec(memory_space=pl.ANY),
        ],
        out_specs=pl.BlockSpec(memory_space=pltpu.VMEM),
        scratch_shapes=[
            pltpu.VMEM((DP, 32, LANES), BF),
            pltpu.VMEM((4, LANES), F32),
            pltpu.VMEM((DP, 32, LANES), BF),
            pltpu.VMEM(gate_up.shape[1:], BF),
            pltpu.VMEM(down.shape[1:], BF),
            pltpu.VMEM((PEERS, 8, LANES), BF),
            pltpu.VMEM((DP, PEERS, 8, LANES), BF),
            pltpu.VMEM((GROUPS, GROUP * 2, QUARTER), BF),
            pltpu.VMEM((GROUPS, DP, GROUP * 2, QUARTER), BF),
            pltpu.VMEM((GROUPS, DP, GROUP * 2, QUARTER), BF),
            pltpu.VMEM((PEERS, 8, LANES), BF),
            pltpu.VMEM((PEERS, 8, LANES), BF),
            pltpu.VMEM((DP, 16, LANES), BF),
            pltpu.VMEM((DP, 16, LANES), BF),
            dma((2,)), dma((3,)), dma((3,)), dma((GROUPS,)), dma((GROUPS,)),
            dma((3, GROUPS)), dma((3, GROUPS)), dma((3, GROUPS)), dma((3, GROUPS)),
            dma, dma, dma((3,)), dma((3,)), dma((2,)),
            pltpu.SemaphoreType.REGULAR, pltpu.SemaphoreType.REGULAR,
            dma((2, GROUPS)), dma((2, GROUPS)),
            pltpu.VMEM((GROUPS, 2, GROUP, QUARTER), BF),
            dma((2, GROUPS)), dma((2, GROUPS)), dma((2, GROUPS)), dma((2, GROUPS)),
        ],
        compiler_params=pltpu.CompilerParams(collective_id=0, has_side_effects=True),
        name="routed_experts",
    )(tokens[0], dest_ids[0], gate_fixed[0], gate_up[0], down[0])
    return out[None]


def solution(mesh):
    return jax.shard_map(
        per_device,
        mesh=mesh,
        in_specs=(
            P("ep", "dp", None),
            P("ep", "dp", None),
            P("ep", "dp", None),
            P("ep", None, "dp", None),
            P("ep", "dp", None),
        ),
        out_specs=P("ep", "dp", None),
        check_vma=False,
    )
```

```python
import jax
import jax.numpy as jnp
from jax import lax
from jax.experimental import pallas as pl
from jax.experimental.pallas import tpu as pltpu
from jax.sharding import PartitionSpec as P

BF = jnp.bfloat16
F32 = jnp.float32
MESH = pl.DeviceIdType.MESH
PEERS = 128
DP = 4
TOP = 8
LANES = 128
QUARTER = 512
STRIDE = 43
GROUPS = 2
GROUP = PEERS // GROUPS


def iota(shape, dim):
    return lax.broadcasted_iota(jnp.int32, shape, dim)


def permutation(inverse):
    moved = iota((128, 128), 1 if inverse else 0)
    place = iota((128, 128), 0 if inverse else 1)
    home = (moved & 31) // 2 * 8 + (moved & 1) * 4 + moved // 32
    return jnp.where(home == place, 1.0, 0.0).astype(BF)


def remote(src, dst, send_sem, recv_sem, device):
    return pltpu.make_async_remote_copy(
        src_ref=src, dst_ref=dst, send_sem=send_sem, recv_sem=recv_sem,
        device_id=device, device_id_type=MESH,
    )


def kernel(
    tokens_ref, ids_ref, gates_ref, pair_hbm, lower_hbm, out_ref,
    msg, table_ref, got, pair, lower, send1, recv1, rows, part, pin, send2, back, outp, fin,
    local_sem, xs, xr, a_send, a_recv, gs, gr, rs, rr, b_send, b_recv, fs, fr, own_sem, line_sem, twin_sem, hs, hr,
    hop, us, ur, ws, wr,
):
    q = lax.axis_index("dp")
    me = lax.axis_index("ep")
    load_pair = pltpu.make_async_copy(pair_hbm, pair, local_sem.at[0])
    load_lower = pltpu.make_async_copy(lower_hbm, lower, local_sem.at[1])
    load_pair.start()
    load_lower.start()

    barrier = pltpu.get_barrier_semaphore()
    for d in range(1, DP):
        pl.semaphore_signal(
            barrier, inc=1, device_id={"dp": lax.rem(q + d, DP)}, device_id_type=MESH
        )

    z, y, core = me // 16, me // 2 % 8, me % 2
    line = [lax.rem(me + 16 * d, PEERS) for d in range(1, 8)]
    across = [z * 16 + lax.rem(y + d, 8) * 2 + core for d in range(1, 8)]
    twin = z * 16 + y * 2 + (1 - core)
    for to in line + across + [twin]:
        pl.semaphore_signal(barrier, inc=1, device_id={"ep": to}, device_id_type=MESH)

    table_ref[...] = jnp.zeros(table_ref.shape, F32)
    table_ref[:, 0:TOP] = ids_ref[...].astype(F32)
    table_ref[:, TOP : 2 * TOP] = (gates_ref[...] >> 8).astype(F32)
    table_ref[:, 2 * TOP : 3 * TOP] = (gates_ref[...] & 255).astype(F32)
    routes = jnp.concatenate([table_ref[...]] * 4, axis=0).astype(BF)
    for i in range(DP):
        pieces = [
            tokens_ref[:, i * QUARTER + j * LANES : i * QUARTER + (j + 1) * LANES].astype(F32)
            for j in range(4)
        ]
        msg[i, 0:16] = jnp.concatenate(pieces, axis=0).astype(BF)
        msg[i, 16:32] = routes
    pl.semaphore_wait(barrier, DP - 1 + 15)
    for to in line:
        pl.semaphore_signal(line_sem, inc=1, device_id={"ep": to}, device_id_type=MESH)
    copies = []
    for d in range(1, DP):
        to = lax.rem(q + d, DP)
        copies.append(
            remote(msg.at[to], got.at[q], xs.at[d - 1], xr.at[d - 1], {"dp": to})
        )
        copies[-1].start()
    got[q] = msg[q]
    pl.semaphore_wait(line_sem, 7)
    pl.semaphore_signal(twin_sem, inc=1, device_id={"ep": twin}, device_id_type=MESH)
    for copy in copies:
        copy.wait()

    tok = jnp.concatenate([got[i, 0:16, :] for i in range(DP)], axis=0)
    table = jnp.concatenate([got[i, 16:32, :].astype(F32) for i in range(DP)], axis=0)
    wide = (64, PEERS * 8)
    column = iota(wide, 1)
    expert = (column // 8).astype(F32)
    named = jnp.zeros(wide, F32)
    high = jnp.zeros(wide, F32)
    low = jnp.zeros(wide, F32)
    total = jnp.zeros((64, 1), F32)
    for k in range(TOP):
        same = table[:, k : k + 1] == expert
        hi, lo = table[:, TOP + k : TOP + k + 1], table[:, 2 * TOP + k : 2 * TOP + k + 1]
        total = total + (hi * 256.0 + lo)
        named = jnp.where(same, 1.0, named)
        high = jnp.where(same, hi, high)
        low = jnp.where(same, lo, low)
    this, other = iota((64, 64), 0), iota((64, 64), 1)
    before = other // 16 * 4 + (other & 3) < this // 16 * 4 + (this & 3)
    earlier = jnp.where(before & ((other // 4 & 3) == 0), 1.0, 0.0).astype(BF)
    rank = jnp.dot(earlier, named.astype(BF), preferred_element_type=F32)
    slot = ((column // 4) & 1).astype(F32)
    live = (rank == slot) & ((iota(wide, 0) // 4 & 3) == (column & 3))
    pick = jnp.where(live, named, 0.0)
    high = jnp.where(live, high, 0.0).astype(BF)
    low = jnp.where(live, low, 0.0).astype(BF)
    packed = jnp.dot(pick.T.astype(BF), tok, preferred_element_type=F32)
    send1[...] = packed.reshape(PEERS, 8, LANES).astype(BF)

    pl.semaphore_wait(twin_sem, 1)

    own = pltpu.make_async_copy(send1.at[me], recv1.at[q, 0], own_sem.at[0])
    own.start()
    for g in range(GROUPS):

        def dispatch(i, carry):
            to = lax.rem(me + i * STRIDE, PEERS)
            remote(send1.at[to], recv1.at[q, i], a_send.at[g], a_recv.at[g], {"ep": to}).start()
            return carry

        lax.fori_loop(max(1, g * GROUP), (g + 1) * GROUP, dispatch, 0)
    own.wait()

    gathers = {}
    relays = {}
    half = GROUP // 2

    def relay(g):
        for d in (1, 3):
            gathers[g, d].wait_recv()
            src = lax.rem(q + DP - d, DP)
            span = pl.ds(g * GROUP + (0 if d == 1 else half), half)
            relays[g, d] = remote(
                recv1.at[src, span], recv1.at[src, span], hs.at[d // 2, g], hr.at[d // 2, g],
                {"dp": lax.rem(q + d, DP)},
            )
            relays[g, d].start()

    for g in range(GROUPS):
        first = max(1, g * GROUP)
        span = pl.ds(first, (g + 1) * GROUP - first)
        remote(
            send1.at[span], recv1.at[q, span], a_send.at[g], a_recv.at[g],
            {"ep": lax.rem(me + 1, PEERS)},
        ).wait()
        span = pl.ds(g * GROUP, GROUP)
        for d in (1, 3):
            to = lax.rem(q + d, DP)
            gathers[g, d] = remote(
                recv1.at[q, span], recv1.at[q, span], gs.at[d - 1, g], gr.at[d - 1, g], {"dp": to}
            )
            gathers[g, d].start()
        if g:
            relay(g - 1)
    load_pair.wait()
    load_lower.wait()
    order = permutation(False)
    back_order = permutation(True)
    contract = (((1,), (1,)), ((), ()))
    reduces, hops, sums = {}, {}, {}
    first_half, second_half = pl.ds(0, GROUP), pl.ds(GROUP, GROUP)

    def experts(g):
        gate = jnp.zeros((GROUP * 2, pair.shape[1]), F32)
        upper = jnp.zeros((GROUP * 2, pair.shape[1]), F32)
        for d in (0, 1, 3, 2):
            if g == 0 and d == 1:
                relay(GROUPS - 1)
            if d == 2:
                for copy in (relays[g, 1], relays[g, 3]):
                    copy.wait()
            elif d:
                gathers[g, d].wait_send()
            src = lax.rem(q + DP - d, DP)
            blocks = []
            for b in range(GROUP // 16):
                start = g * GROUP + b * 16
                block = recv1[src, start : start + 16].astype(F32).reshape(128, LANES)
                blocks.append(block.astype(BF))
            moved = jnp.dot(
                order, jnp.concatenate(blocks, axis=1), preferred_element_type=F32
            ).astype(BF)
            for b in range(GROUP // 16):
                for j in range(4):
                    rows[g, b * 32 : (b + 1) * 32, j * LANES : (j + 1) * LANES] = moved[
                        j * 32 : (j + 1) * 32, b * LANES : (b + 1) * LANES
                    ]
            x = rows[g]
            features = pl.ds(pl.multiple_of(src * QUARTER, QUARTER), QUARTER)
            gate = gate + lax.dot_general(
                x, pair[0, :, features], contract, preferred_element_type=F32
            )
            upper = upper + lax.dot_general(
                x, pair[1, :, features], contract, preferred_element_type=F32
            )
        if g:
            relay_sum(g - 1)
        hidden = (gate / (1.0 + jnp.exp(-gate)) * upper).astype(BF)
        for d in (2, 1, 3, 0):
            to = lax.rem(q + d, DP)
            features = pl.ds(pl.multiple_of(to * QUARTER, QUARTER), QUARTER)
            part[g, to] = jnp.dot(hidden, lower[:, features], preferred_element_type=F32).astype(BF)
            for side in (1, 3):
                if d == 2:
                    lines = first_half if side == 1 else second_half
                    hops[g, side] = remote(
                        part.at[g, to, lines], hop.at[g, side // 2],
                        us.at[side // 2, g], ur.at[side // 2, g], {"dp": lax.rem(q + side, DP)},
                    )
                    hops[g, side].start()
                elif d == side:
                    lines = second_half if side == 1 else first_half
                    reduces[g, d] = remote(
                        part.at[g, to, lines], pin.at[g, q, lines],
                        rs.at[d - 1, g], rr.at[d - 1, g], {"dp": to},
                    )
                    reduces[g, d].start()

    def relay_sum(g):
        for d in (1, 3):
            hops[g, d].wait()
            to = lax.rem(q + d, DP)
            lines = first_half if d == 1 else second_half
            both = part[g, to, lines].astype(F32) + hop[g, d // 2].astype(F32)
            part[g, to, lines] = both.astype(BF)
            sums[g, d] = remote(
                part.at[g, to, lines], pin.at[g, q, lines],
                ws.at[d // 2, g], wr.at[d // 2, g], {"dp": to},
            )
            sums[g, d].start()

    def finish(g):
        for d in (1, 3):
            reduces[g, d].wait()
            sums[g, d].wait()
        blocks = []
        for b in range(GROUP // 16):
            lines = slice(b * 32, (b + 1) * 32)
            added = part[g, q, lines].astype(F32)
            for d in (1, 3):
                added = added + pin[g, lax.rem(q + DP - d, DP), lines].astype(F32)
            added = added.astype(BF)
            blocks.append(
                jnp.concatenate([added[:, j * LANES : (j + 1) * LANES] for j in range(4)], axis=0)
            )
        moved = jnp.dot(
            back_order, jnp.concatenate(blocks, axis=1), preferred_element_type=F32
        )
        for b in range(GROUP // 16):
            start = g * GROUP + b * 16
            block = moved[:, b * LANES : (b + 1) * LANES]
            send2[start : start + 16] = block.reshape(16, 8, LANES).astype(BF)

        def giveback(i, carry):
            to = lax.rem(me + i * (PEERS - STRIDE), PEERS)
            remote(send2.at[i], back.at[me], b_send, b_recv, {"ep": to}).start()
            return carry

        lax.fori_loop(max(1, g * GROUP), (g + 1) * GROUP, giveback, 0)

    for g in range(GROUPS):
        experts(g)
        if g:
            finish(g - 1)
    relay_sum(GROUPS - 1)
    own = pltpu.make_async_copy(send2.at[0], back.at[me], own_sem.at[1])
    own.start()
    finish(GROUPS - 1)
    own.wait()
    whole = pl.ds(0, PEERS - 1)
    remote(
        send2.at[whole], back.at[whole], b_send, b_recv, {"ep": lax.rem(me + 1, PEERS)}
    ).wait()

    results = back[...].astype(F32).reshape(PEERS * 8, LANES).astype(BF)
    mixed = jnp.dot(high, results, preferred_element_type=F32) * 256.0
    mixed = mixed + jnp.dot(low, results, preferred_element_type=F32)
    mixed = (mixed / total).astype(BF)
    for i in range(DP):
        outp[i] = mixed[i * 16 : (i + 1) * 16]
    copies = []
    for d in range(1, DP):
        to = lax.rem(q + d, DP)
        copies.append(remote(outp.at[to], fin.at[q], fs.at[d - 1], fr.at[d - 1], {"dp": to}))
        copies[-1].start()
    for d in range(DP):
        if d:
            copies[d - 1].wait()
        src = lax.rem(q + DP - d, DP)
        value = (fin[src] if d else outp[q]).astype(F32)
        for j in range(4):
            features = pl.ds(pl.multiple_of(src * QUARTER + j * LANES, LANES), LANES)
            out_ref[:, features] = value[j * 4 : (j + 1) * 4].astype(BF)


def per_device(tokens, dest_ids, gate_fixed, gate_up, down):
    dma = pltpu.SemaphoreType.DMA
    out = pl.pallas_call(
        kernel,
        out_shape=jax.ShapeDtypeStruct((4, DP * QUARTER), BF),
        in_specs=[
            pl.BlockSpec(memory_space=pltpu.VMEM),
            pl.BlockSpec(memory_space=pltpu.VMEM),
            pl.BlockSpec(memory_space=pltpu.VMEM),
            pl.BlockSpec(memory_space=pl.ANY),
            pl.BlockSpec(memory_space=pl.ANY),
        ],
        out_specs=pl.BlockSpec(memory_space=pltpu.VMEM),
        scratch_shapes=[
            pltpu.VMEM((DP, 32, LANES), BF),
            pltpu.VMEM((4, LANES), F32),
            pltpu.VMEM((DP, 32, LANES), BF),
            pltpu.VMEM(gate_up.shape[1:], BF),
            pltpu.VMEM(down.shape[1:], BF),
            pltpu.VMEM((PEERS, 8, LANES), BF),
            pltpu.VMEM((DP, PEERS, 8, LANES), BF),
            pltpu.VMEM((GROUPS, GROUP * 2, QUARTER), BF),
            pltpu.VMEM((GROUPS, DP, GROUP * 2, QUARTER), BF),
            pltpu.VMEM((GROUPS, DP, GROUP * 2, QUARTER), BF),
            pltpu.VMEM((PEERS, 8, LANES), BF),
            pltpu.VMEM((PEERS, 8, LANES), BF),
            pltpu.VMEM((DP, 16, LANES), BF),
            pltpu.VMEM((DP, 16, LANES), BF),
            dma((2,)), dma((3,)), dma((3,)), dma((GROUPS,)), dma((GROUPS,)),
            dma((3, GROUPS)), dma((3, GROUPS)), dma((3, GROUPS)), dma((3, GROUPS)),
            dma, dma, dma((3,)), dma((3,)), dma((2,)),
            pltpu.SemaphoreType.REGULAR, pltpu.SemaphoreType.REGULAR,
            dma((2, GROUPS)), dma((2, GROUPS)),
            pltpu.VMEM((GROUPS, 2, GROUP, QUARTER), BF),
            dma((2, GROUPS)), dma((2, GROUPS)), dma((2, GROUPS)), dma((2, GROUPS)),
        ],
        compiler_params=pltpu.CompilerParams(collective_id=0, has_side_effects=True),
        name="routed_experts",
    )(tokens[0], dest_ids[0], gate_fixed[0], gate_up[0], down[0])
    return out[None]


def solution(mesh):
    return jax.shard_map(
        per_device,
        mesh=mesh,
        in_specs=(
            P("ep", "dp", None),
            P("ep", "dp", None),
            P("ep", "dp", None),
            P("ep", None, "dp", None),
            P("ep", "dp", None),
        ),
        out_specs=P("ep", "dp", None),
        check_vma=False,
    )
```
